32 devices in a mesh: beams: 2 (over x), tm: 16 (over z, y, core).
Axes of the slice: x: 2, y: 2, z: 4, core: 2. Of those that a mesh axis runs over, the one named last changes fastest.
Arguments:
- samples: bfloat16 [2048, 8192], P('tm', 'beams'), parts along dimension 1, may hold values from -2400 to 2400
- channel_band: int32 [4096], replicated, may hold values from 0 to 15, never falling along the last dimension, each value on 1 to 512 neighbouring positions
- delays: int32 [16, 4096], replicated, may hold values from 0 to 8192, as said below
- template_bank: bfloat16 [2, 128, 256], replicated, may hold values from -0.25 to 0.25
- template_ids: int32 [64], replicated, may hold values from 0 to 127
Outputs:
- powers: float32 [32, 64, 2048], P('beams', None, 'tm'), parts along dimension 0
The draws below stay inside these ranges and needn't reach their ends.
There are 2 independent parts, one for each index of `beams`. The reference program is written for one: setup_inputs(seed, part) draws one part's arguments, and reference() takes and returns one part's arrays. A program takes and returns all parts, laid end to end along the dimension named above; an argument that names none is the same for every part. Nothing has to cross between parts.
Inputs may be any that keep to these rules, and one draw needn't show every extreme that they name: `channel_band`: band numbers never fall along the channels and every band holds at least one channel. delays never rise along the channels and never fall from one trial to the next; the last channel's delays are 0.
All inputs are finite; a program needn't handle non-finite values.
Results may differ from the reference program's by a relative error of at most 0.0061.
Values may be sent and summed in bfloat16 or wider, within the bound.
A program may use at most 128 MiB of HBM per device.

```python
import math
import jax
import jax.numpy as jnp
import numpy as np
from jax import lax

CH = 4096
NB = 16
T_DEV = 128
TR = 16
NZ = 64
TAPS = 256
NBANK = 128
SUB = 16
NT = 2048
DLIM = 8192
N_TM = 16


measure_top = 16384


def draw_samples(key, part):
    noise_key, row_key, column_key = jax.random.split(key, 3)
    time_pos = jnp.arange(NT, dtype=jnp.float32) / NT
    chan_pos = jnp.arange(CH, dtype=jnp.float32) / CH
    row_jitter = jax.random.uniform(row_key, (NT,), jnp.float32, 1.0, 2.0)
    column_jitter = jax.random.uniform(column_key, (CH,), jnp.float32, 1.0, 2.0)
    noise_values = jax.random.truncated_normal(noise_key, -6.0, 6.0, (NT, CH), jnp.float32)
    row_scale = 10.0 ** time_pos
    column_scale = 10.0 ** (1.0 - chan_pos)
    scaled = noise_values * (row_scale * row_jitter)[:, None] * (column_scale * column_jitter)[None, :]
    return scaled.astype(jnp.bfloat16)


def draw_delays(key, part):
    jitter_key = jax.random.fold_in(key, 31)
    channel = jnp.arange(CH, dtype=jnp.int32)
    frequency = 4 * CH + 1 + channel
    below_top = 5 * CH - frequency
    above_sum = 5 * CH + frequency
    ratio_low = below_top * 32768 // frequency
    ratio_high = above_sum * 8192 // frequency
    curve = ratio_low * ratio_high // 8192
    base_delay = DLIM * curve // curve[0]
    trial = jnp.arange(TR, dtype=jnp.int32)
    jitter = jax.random.randint(jitter_key, (TR,), 0, measure_top // (2 * TR), dtype=jnp.int32)
    measure = measure_top * (trial + 1) // TR - jitter
    measure = jnp.where(trial == TR - 1, measure_top, measure)
    return (measure[:, None] * base_delay[None, :] // measure_top).astype(jnp.int32)


def plant(entries, key, smallest, high):
    dims = entries.shape
    place = [jax.random.randint(jax.random.fold_in(key, axis), (), 0, dims[axis]) for axis in range(len(dims))]
    entries = entries.at[tuple(place)].set(smallest)
    longest = dims.index(max(dims))
    place[longest] = (place[longest] + 1) % dims[longest]
    return entries.at[tuple(place)].set(high)


def profile(number_of, total, reach, skew):
    loads = [(1 << 20) // math.isqrt(rank ** skew) + 1 for rank in range(2, number_of + 1)]
    rest, counts = total - reach - (number_of - 1), [1] * (number_of - 1)
    while rest > 0:
        free = [i for i in range(number_of - 1) if counts[i] < reach]
        whole, budget = sum([loads[i] for i in free]), rest
        for i in free:
            addition = min(reach - counts[i], max(1, budget * loads[i] // whole), rest)
            counts[i] = counts[i] + addition
            rest = rest - addition
    return np.array([reach] + counts)


def uneven(stream_key, number_of, total, bound, skew):
    if number_of == 2:
        one = jax.random.randint(stream_key, (), max(1, total - bound), min(bound, total - 1) + 1)
        return jnp.stack([one, total - one])
    sizes = jnp.asarray(profile(number_of, total, bound, skew), jnp.int32)
    couples = (number_of - 1) // 2
    giver, taker = sizes[1:1 + 2 * couples:2], sizes[2:2 + 2 * couples:2]
    margin = jnp.minimum(giver - 1, bound - taker)
    shifted = jax.random.randint(jax.random.fold_in(stream_key, 1), (couples,), 0, 1 << 20) % (margin + 1)
    sizes = sizes.at[1:1 + 2 * couples:2].set(giver - shifted).at[2:2 + 2 * couples:2].set(taker + shifted)
    return sizes[jax.random.permutation(jax.random.fold_in(stream_key, 2), number_of)]


def noise(key, dims, spread, limit, held_as=jnp.bfloat16):
    entries = jax.random.normal(key, dims, jnp.float32) * spread
    return jnp.minimum(jnp.maximum(entries, -limit), limit).astype(held_as)


def setup_inputs(seed: int = 0, part: int = 0) -> dict:
    seeds = jax.random.split(jax.random.key(seed), 6)
    part_keys = jax.random.split(jax.random.fold_in(seeds[5], part), 6)
    samples = draw_samples(jax.random.fold_in(jax.random.fold_in(seeds[5], part), 71), part)
    channel_band = jnp.searchsorted(jnp.cumsum(uneven(seeds[1], NB, CH, 2 * CH // NB, 0)), jnp.arange(CH), side="right").astype(jnp.int32)
    delays = draw_delays(jax.random.fold_in(seeds[5], 71), part)
    template_bank = noise(seeds[3], (2, NBANK, TAPS), (2 * TAPS) ** -0.5, 0.25)
    template_ids = plant(jax.random.randint(seeds[4], (NZ,), 0, NBANK), jax.random.fold_in(seeds[4], 1), 0, NBANK - 1).astype(jnp.int32)
    return dict(samples=samples, channel_band=channel_band, delays=delays, template_bank=template_bank, template_ids=template_ids)


full_turn = 2.0 * math.pi

def dft_table(length):
    index_row = jnp.arange(length, dtype=jnp.int32)
    turn_count = index_row[:, None] * index_row[None, :] % length
    phase_angle = turn_count.astype(jnp.float32) * (full_turn / length)
    return (jnp.cos(phase_angle).astype(jnp.bfloat16), (-jnp.sin(phase_angle)).astype(jnp.bfloat16))

def phase_sum(spec_real, spec_imag, bin_index, lag_row, weight, sum_axis, period):
    turn_count = bin_index * lag_row % period
    phase_angle = turn_count.astype(jnp.float32) * (full_turn / period)
    cosine = jnp.cos(phase_angle) * weight
    sine_part = jnp.sin(phase_angle) * weight
    real_part = spec_real.astype(jnp.float32)
    imag_part = spec_imag.astype(jnp.float32)
    return (lax.optimization_barrier(jnp.sum(cosine * real_part - sine_part * imag_part, axis=sum_axis)), lax.optimization_barrier(jnp.sum(sine_part * real_part + cosine * imag_part, axis=sum_axis)))

def reference(samples, channel_band, delays, template_bank, template_ids):
    squares = lax.optimization_barrier(jnp.sum(jnp.square(samples.astype(jnp.float32)), axis=0))
    onehot = (channel_band[:, None] == jnp.arange(NB, dtype=jnp.int32)[None, :]).astype(jnp.float32)
    band_power = jnp.dot(squares, onehot, precision=lax.Precision.HIGHEST)
    members = lax.optimization_barrier(jnp.sum(onehot, axis=0))
    mean_square = band_power / (members * NT)
    band_gain = 1.0 / (jnp.sqrt(mean_square + 1e-06) * math.sqrt(CH * NT))
    gains = band_gain[channel_band]
    fp_real, fp_imag = dft_table(N_TM)
    left_matrix = samples.reshape(N_TM, T_DEV * CH)
    z_real = jnp.dot(fp_real, left_matrix, preferred_element_type=jnp.float32).reshape(N_TM, T_DEV, CH)
    z_imag = jnp.dot(fp_imag, left_matrix, preferred_element_type=jnp.float32).reshape(N_TM, T_DEV, CH)
    freq_part = jnp.arange(N_TM, dtype=jnp.int32)
    time_part = jnp.arange(T_DEV, dtype=jnp.int32)
    twist = (freq_part[:, None] * time_part[None, :] % NT).astype(jnp.float32) * (full_turn / NT)
    twist_cos = jnp.cos(twist)[:, :, None]
    twist_sin = jnp.sin(twist)[:, :, None]
    y_real = (z_real * twist_cos + z_imag * twist_sin).astype(jnp.bfloat16)
    y_imag = (z_imag * twist_cos - z_real * twist_sin).astype(jnp.bfloat16)
    fs_real, fs_imag = dft_table(T_DEV)
    flat_real = y_real.transpose(1, 0, 2).reshape(T_DEV, N_TM * CH)
    flat_imag = y_imag.transpose(1, 0, 2).reshape(T_DEV, N_TM * CH)
    x_real = (jnp.dot(fs_real, flat_real, preferred_element_type=jnp.float32) - jnp.dot(fs_imag, flat_imag, preferred_element_type=jnp.float32)).astype(jnp.bfloat16).reshape(NT, CH)
    x_imag = (jnp.dot(fs_real, flat_imag, preferred_element_type=jnp.float32) + jnp.dot(fs_imag, flat_real, preferred_element_type=jnp.float32)).astype(jnp.bfloat16).reshape(NT, CH)
    block_len = math.gcd(NT, 2048)
    block_count = NT // block_len
    all_bins = jnp.arange(NT, dtype=jnp.int32).reshape(block_count, block_len)
    x_real_blocks = x_real.reshape(block_count, block_len, CH)
    x_imag_blocks = x_imag.reshape(block_count, block_len, CH)
    period = SUB * NT

    def one_trial(lag_row):

        def one_block(pieces):
            part_real, part_imag, bin_index = pieces
            return phase_sum(part_real, part_imag, bin_index[:, None], lag_row[None, :], gains[None, :], 1, period)
        out_real, out_imag = lax.map(one_block, (x_real_blocks, x_imag_blocks, all_bins))
        return (out_real.reshape(NT), out_imag.reshape(NT))
    d_real, d_imag = lax.map(one_trial, delays)
    d_real = d_real.astype(jnp.bfloat16)
    d_imag = d_imag.astype(jnp.bfloat16)
    picked = template_bank[:, template_ids, :]
    h_real = picked[0].T
    h_imag = picked[1].T
    offsets = (jnp.arange(NT, dtype=jnp.int32)[:, None] + jnp.arange(TAPS, dtype=jnp.int32)[None, :] - TAPS // 2) % NT

    def one_plane(pieces):
        row_real, row_imag = pieces
        u_real = row_real[offsets]
        u_imag = row_imag[offsets]
        a_real = jnp.dot(u_real, h_real, preferred_element_type=jnp.float32) - jnp.dot(u_imag, h_imag, preferred_element_type=jnp.float32)
        a_imag = jnp.dot(u_real, h_imag, preferred_element_type=jnp.float32) + jnp.dot(u_imag, h_real, preferred_element_type=jnp.float32)
        return (a_real * a_real + a_imag * a_imag).T
    return lax.map(one_plane, (d_real, d_imag))
```

```python
import functools
import math

import jax
import jax.numpy as jnp
from jax import lax
from jax.experimental import pallas as pl
from jax.experimental.pallas import tpu as pltpu
from jax.sharding import PartitionSpec as P

NB = 16
SUB = 16
CB = 256
VB = 256
UNROLL = 8
LANES = 128
full_turn = 2.0 * math.pi


def spread_kernel(n_ref, code_ref, s_ref, lag_ref, g_ref, out_ref, acc_ref):
    rows = s_ref.shape[1]
    groups = rows // 8
    tiles = groups + VB // LANES - 1
    acc_ref[...] = jnp.zeros_like(acc_ref)
    step_row = lax.broadcasted_iota(jnp.int32, (VB, CB), 0)

    def body(it, carry):
        for j in range(UNROLL):
            code = code_ref[it * UNROLL + j]
            d = code & 31
            cb = (code >> 5) & 31
            vt = code >> 10
            lag = lag_ref[cb, pl.ds(d, 1), :] - vt * VB
            hot = jnp.where(step_row == lag, g_ref[cb], 0.0).astype(jnp.bfloat16)
            res = lax.dot_general(
                s_ref[cb], hot, (((1,), (1,)), ((), ())), preferred_element_type=jnp.float32
            )
            parts = []
            for tile in range(tiles):
                total = None
                for half in range(VB // LANES):
                    g = tile - half
                    if 0 <= g < groups:
                        piece = res[8 * g : 8 * g + 8, half * LANES : (half + 1) * LANES]
                        total = piece if total is None else total + piece
                parts.append(total)
            cols = pl.ds(pl.multiple_of(vt * VB, VB), tiles * LANES)
            acc_ref[d, :, cols] += jnp.concatenate(parts, axis=1)
        return carry

    lax.fori_loop(0, n_ref[0], body, 0)

    def finish(d, carry):
        x = acc_ref[d]
        x = pltpu.roll(x, 0, 1, stride=SUB, stride_axis=0)
        out_ref[pl.ds(d, 1), :] = jnp.sum(x, axis=0, keepdims=True)
        return carry

    lax.fori_loop(0, acc_ref.shape[0], finish, 0)


def conv_kernel(h_ref, re_ref, im_ref, out_ref):
    taps = h_ref.shape[1]
    nz = h_ref.shape[0] // 2
    trials, span = re_ref.shape
    width = span - taps

    def body(d, carry):
        cols = []
        for ref in (re_ref, im_ref):
            x = jnp.broadcast_to(ref[pl.ds(d, 1), :], (taps, span))
            x = pltpu.roll(x, span - taps + 1, 1, stride=1, stride_axis=0)
            cols.append(x[:, :width].astype(jnp.bfloat16))
        res = jnp.dot(h_ref[...], jnp.concatenate(cols, axis=1), preferred_element_type=jnp.float32)
        a_re = res[:nz, :width] - res[nz:, width:]
        a_im = res[:nz, width:] + res[nz:, :width]
        out_ref[d] = a_re * a_re + a_im * a_im
        return carry

    lax.fori_loop(0, trials, body, 0)


def per_device(samples, channel_band, delays, template_bank, template_ids):
    rows, channels = samples.shape
    trials = delays.shape[0]
    devices = lax.axis_size("tm")
    bins = rows * devices
    period = SUB * bins
    top = bins * 4
    own = lax.axis_index("tm")

    squares = jnp.sum(jnp.square(samples.astype(jnp.float32)), axis=0)
    onehot = (channel_band[:, None] == jnp.arange(NB, dtype=jnp.int32)[None, :]).astype(jnp.float32)
    local_power = jnp.dot(squares, onehot, precision=lax.Precision.HIGHEST)
    all_power = lax.all_to_all(
        jnp.broadcast_to(local_power[None], (devices, NB)), "tm", split_axis=0, concat_axis=0, tiled=True
    )
    band_power = jnp.sum(all_power, axis=0)
    members = jnp.sum(onehot, axis=0)
    band_gain = 1.0 / (
        jnp.sqrt(band_power / (members * bins) + 1e-06) * math.sqrt(channels * bins)
    )
    gains = jnp.dot(onehot, band_gain, precision=lax.Precision.HIGHEST)

    blocks = channels // CB
    lag = top - delays
    lag3 = lag.reshape(trials, blocks, CB)
    first = (lag3[:, :, 0] // VB).reshape(-1)
    last = (lag3[:, :, CB - 1] // VB).reshape(-1)
    count = last - first + 1
    ends = jnp.cumsum(count)
    starts = ends - count
    spare = top // VB + 1
    most = trials * (blocks + spare)
    most = -(-most // UNROLL) * UNROLL
    item = jnp.arange(most, dtype=jnp.int32)
    pair = jnp.sum((item[:, None] >= ends[None, :]).astype(jnp.int32), axis=1)
    inside = pair < trials * blocks
    hit = pair[:, None] == jnp.arange(trials * blocks, dtype=jnp.int32)[None, :]
    base = jnp.sum(jnp.where(hit, (first - starts)[None, :], 0), axis=1)
    tile = jnp.where(inside, base + item, spare)
    pair = jnp.where(inside, pair, 0)
    code = (pair // blocks) + 32 * (pair % blocks) + 1024 * tile
    n_iter = (ends[-1:] + (UNROLL - 1)) // UNROLL

    width = (spare + 1) * VB + SUB * rows
    smem = pl.BlockSpec(memory_space=pltpu.SMEM)
    vmem = pl.BlockSpec(memory_space=pltpu.VMEM)
    series = pl.pallas_call(
        spread_kernel,
        out_shape=jax.ShapeDtypeStruct((trials, width), jnp.float32),
        in_specs=[smem, smem, vmem, vmem, vmem],
        out_specs=vmem,
        scratch_shapes=[pltpu.VMEM((trials, 8, width), jnp.float32)],
        name="spread",
    )(
        n_iter,
        code,
        samples.reshape(rows, blocks, CB).transpose(1, 0, 2),
        lag3.transpose(1, 0, 2),
        gains.reshape(blocks, 1, CB),
    )

    outer = width // LANES
    inner = bins * SUB // LANES
    reps = bins // inner
    k1 = jnp.arange(inner, dtype=jnp.int32)
    a = jnp.arange(outer, dtype=jnp.int32)
    b = jnp.arange(LANES, dtype=jnp.int32)
    k2 = jnp.arange(reps, dtype=jnp.int32)
    ang1 = (k1[:, None] * a[None, :] % inner).astype(jnp.float32) * (full_turn / inner)
    t3 = series.reshape(trials, outer, LANES)
    tab1 = jnp.stack([jnp.cos(ang1), -jnp.sin(ang1)])
    g = jnp.einsum("ika,dab->ikdb", tab1, t3, precision=lax.Precision.HIGH)
    ang2 = (k1[:, None] * b[None, :]).astype(jnp.float32) * (full_turn / period)
    c2, s2 = jnp.cos(ang2)[:, None, :], jnp.sin(ang2)[:, None, :]
    gr = g[0] * c2 + g[1] * s2
    gi = g[1] * c2 - g[0] * s2
    ang3 = (k2[:, None] * b[None, :] % LANES).astype(jnp.float32) * (full_turn / LANES)
    c3, s3 = jnp.cos(ang3), jnp.sin(ang3)
    gcat = jnp.concatenate([gr, gi], axis=2)
    tab3 = jnp.stack([jnp.concatenate([c3, s3], axis=1), jnp.concatenate([-s3, c3], axis=1)])
    d2 = jnp.einsum("kdb,irb->idrk", gcat, tab3, precision=lax.Precision.HIGH)
    d2 = d2.reshape(2, trials, bins)
    kk = jnp.arange(bins, dtype=jnp.int32)
    ang4 = (kk * (own * (SUB * rows) - top) % period).astype(jnp.float32) * (full_turn / period)
    c4, s4 = jnp.cos(ang4), jnp.sin(ang4)
    part = jnp.stack([d2[0] * c4 + d2[1] * s4, d2[1] * c4 - d2[0] * s4]).astype(jnp.bfloat16)

    taps = template_bank.shape[2]
    half = taps // 2
    split = part.reshape(2, trials, devices, rows)
    wide = jnp.concatenate([jnp.roll(split, 1, axis=2)[..., rows - half:], split, jnp.roll(split, -1, axis=2)[..., :half]], axis=3)
    moved = lax.all_to_all(wide.transpose(2, 0, 1, 3), "tm", split_axis=0, concat_axis=0, tiled=True)
    ded = jnp.sum(moved.astype(jnp.float32), axis=0).astype(jnp.bfloat16).astype(jnp.float32)

    nz = template_ids.shape[0]
    selector = (template_ids[:, None] == jnp.arange(template_bank.shape[1], dtype=jnp.int32)[None, :]).astype(jnp.bfloat16)
    chosen = jnp.einsum("zb,ibt->izt", selector, template_bank[:, :, ::-1], preferred_element_type=jnp.float32)
    chosen = chosen.astype(jnp.bfloat16).reshape(2 * nz, taps)
    return pl.pallas_call(
        conv_kernel,
        out_shape=jax.ShapeDtypeStruct((trials, nz, rows), jnp.float32),
        in_specs=[vmem, vmem, vmem],
        out_specs=vmem,
        name="conv",
    )(chosen, ded[0], ded[1])


def solution(mesh):
    return jax.shard_map(
        per_device,
        mesh=mesh,
        in_specs=(P("tm", "beams"), P(), P(), P(), P()),
        out_specs=P("beams", None, "tm"),
        check_vma=False,
    )
```

```python
import functools
import math

import jax
import jax.numpy as jnp
from jax import lax
from jax.experimental import pallas as pl
from jax.experimental.pallas import tpu as pltpu
from jax.sharding import PartitionSpec as P

NB = 16
SUB = 16
CB = 256
VB = 128
UNROLL = 16
LANES = 128
MESH = pl.DeviceIdType.MESH
full_turn = 2.0 * math.pi


def spread_kernel(n_ref, code_ref, s_ref, lag_ref, g_ref, out_ref, acc_ref, scaled_ref):
    rows, channels = s_ref.shape
    groups = rows // 8
    acc_ref[...] = jnp.zeros_like(acc_ref)
    lane = lax.broadcasted_iota(jnp.int32, (CB, VB), 1).astype(jnp.float32).astype(jnp.bfloat16)
    one = jnp.ones((CB, VB), jnp.bfloat16)
    zero = jnp.zeros((CB, VB), jnp.bfloat16)

    def scale(cb, carry):
        cols = pl.ds(pl.multiple_of(cb * CB, CB), CB)
        scaled_ref[:, cols] = (s_ref[:, cols].astype(jnp.float32) * g_ref[:, cols]).astype(jnp.bfloat16)
        return carry

    lax.fori_loop(0, channels // CB, scale, 0)

    def body(it, carry):
        for j in range(UNROLL):
            places, hots = [], []
            for half in range(2):
                code = code_ref[(it * UNROLL + j) * 2 + half]
                d = code & 31
                cb = (code >> 5) & 31
                vt = code >> 10
                cols = pl.ds(pl.multiple_of(cb * CB, CB), CB)
                lag = (lag_ref[pl.ds(d, 1), cols] - vt * VB).astype(jnp.float32)
                lag = jnp.broadcast_to(lag, (VB, CB)).T.astype(jnp.bfloat16)
                hots.append(jnp.where(lag == lane, one, zero))
                places.append((d, vt))
            res = jnp.dot(
                scaled_ref[:, cols],
                jnp.concatenate(hots, axis=1),
                preferred_element_type=jnp.float32,
            )
            for half, (d, vt) in enumerate(places):
                wide = jnp.concatenate(
                    [res[8 * g : 8 * g + 8, half * VB : (half + 1) * VB] for g in range(groups)], axis=1
                )
                at = pl.ds(pl.multiple_of(vt * VB, VB), groups * VB)
                acc_ref[d, :, at] += wide
        return carry

    lax.fori_loop(0, n_ref[0], body, 0)

    def finish(d, carry):
        x = acc_ref[d]
        x = pltpu.roll(x, 0, 1, stride=SUB, stride_axis=0)
        out_ref[pl.ds(d, 1), :] = jnp.sum(x, axis=0, keepdims=True)
        return carry

    lax.fori_loop(0, acc_ref.shape[0], finish, 0)


def greet(devices, me):
    barrier = pltpu.get_barrier_semaphore()

    def hello(i, carry):
        pl.semaphore_signal(barrier, inc=1, device_id={"tm": (me + i) % devices}, device_id_type=MESH)
        return carry

    lax.fori_loop(1, devices, hello, 0)
    pl.semaphore_wait(barrier, devices - 1)


def power_kernel(devices, bins, s_ref, band_ref, gain_ref, mine_ref, got_ref, send_sem, recv_sem):
    me = lax.axis_index("tm")
    rows, channels = s_ref.shape
    band = band_ref[...]
    hit = band == lax.broadcasted_iota(jnp.int32, (NB, channels), 0)
    part = 256
    squares = []
    for c in range(0, channels, part):
        x = s_ref[:, c : c + part].astype(jnp.float32)
        squares.append(jnp.sum(x * x, axis=0, keepdims=True))
    squares = jnp.concatenate(squares, axis=1)
    power = jnp.sum(jnp.where(hit, squares, 0.0), axis=1, keepdims=True)
    members = jnp.sum(jnp.where(hit, 1.0, 0.0), axis=1, keepdims=True)
    eye = lax.broadcasted_iota(jnp.int32, (NB, LANES), 0) == lax.broadcasted_iota(jnp.int32, (NB, LANES), 1)
    mine_ref[...] = jnp.sum(jnp.where(eye, power, 0.0), axis=0, keepdims=True)
    greet(devices, me)

    def copy_to(peer, slot):
        return pltpu.make_async_remote_copy(
            src_ref=mine_ref,
            dst_ref=got_ref.at[slot],
            send_sem=send_sem.at[peer],
            recv_sem=recv_sem.at[slot],
            device_id={"tm": peer},
            device_id_type=MESH,
        )

    def send(i, carry):
        copy_to((me + i) % devices, me).start()
        return carry

    lax.fori_loop(1, devices, send, 0)

    def take(i, total):
        q = (me + devices - i) % devices
        copy_to(q, q).wait_recv()
        return total + got_ref[q]

    total = lax.fori_loop(1, devices, take, mine_ref[...])
    column = jnp.sum(jnp.where(eye, total, 0.0), axis=1, keepdims=True)
    band_gain = 1.0 / (jnp.sqrt(column / (members * bins) + 1e-06) * math.sqrt(channels * bins))
    gain_ref[...] = jnp.sum(jnp.where(hit, band_gain, 0.0), axis=0, keepdims=True)

    def sent(i, carry):
        copy_to((me + i) % devices, me).wait_send()
        return carry

    lax.fori_loop(1, devices, sent, 0)


def gather_kernel(devices, half, part_ref, out_ref, got_ref, mine_ref, left_ref, right_ref, send_sem, recv_sem, halo_sem):
    me = lax.axis_index("tm")
    rows = part_ref.shape[2]
    greet(devices, me)

    def copy_to(peer, slot):
        return pltpu.make_async_remote_copy(
            src_ref=part_ref.at[peer],
            dst_ref=got_ref.at[slot],
            send_sem=send_sem.at[peer],
            recv_sem=recv_sem.at[slot],
            device_id={"tm": peer},
            device_id_type=MESH,
        )

    def send(i, carry):
        copy_to((me + i) % devices, me).start()
        return carry

    lax.fori_loop(1, devices, send, 0)

    def take(i, total):
        q = (me + devices - i) % devices
        copy_to(q, q).wait_recv()
        return total + got_ref[q].astype(jnp.float32)

    total = lax.fori_loop(1, devices, take, part_ref[me].astype(jnp.float32)).astype(jnp.bfloat16)
    mine_ref[...] = total
    halos = []
    for n, (peer, source, target) in enumerate(
        (
            ((me + 1) % devices, mine_ref.at[:, rows - half :], left_ref),
            ((me + devices - 1) % devices, mine_ref.at[:, :half], right_ref),
        )
    ):
        copy = pltpu.make_async_remote_copy(
            src_ref=source,
            dst_ref=target,
            send_sem=halo_sem.at[2 * n],
            recv_sem=halo_sem.at[2 * n + 1],
            device_id={"tm": peer},
            device_id_type=MESH,
        )
        copy.start()
        halos.append(copy)
    out_ref[:, half : half + rows] = total.astype(jnp.float32)

    def sent(i, carry):
        copy_to((me + i) % devices, me).wait_send()
        return carry

    lax.fori_loop(1, devices, sent, 0)
    for copy in halos:
        copy.wait()
    out_ref[:, :half] = left_ref[...].astype(jnp.float32)
    out_ref[:, half + rows :] = right_ref[...].astype(jnp.float32)


def conv_kernel(h_ref, re_ref, im_ref, out_ref):
    taps = h_ref.shape[1]
    nz = h_ref.shape[0] // 2
    trials, span = re_ref.shape
    width = span - taps

    def body(d, carry):
        cols = []
        for ref in (re_ref, im_ref):
            x = jnp.broadcast_to(ref[pl.ds(d, 1), :], (taps, span))
            x = pltpu.roll(x, span - taps + 1, 1, stride=1, stride_axis=0)
            cols.append(x[:, :width].astype(jnp.bfloat16))
        res = jnp.dot(h_ref[...], jnp.concatenate(cols, axis=1), preferred_element_type=jnp.float32)
        a_re = res[:nz, :width] - res[nz:, width:]
        a_im = res[:nz, width:] + res[nz:, :width]
        out_ref[d] = a_re * a_re + a_im * a_im
        return carry

    lax.fori_loop(0, trials, body, 0)


def per_device(samples, channel_band, delays, template_bank, template_ids):
    rows, channels = samples.shape
    trials = delays.shape[0]
    devices = lax.axis_size("tm")
    bins = rows * devices
    period = SUB * bins
    top = bins * 4
    own = lax.axis_index("tm")

    gains = pl.pallas_call(
        functools.partial(power_kernel, devices, bins),
        out_shape=jax.ShapeDtypeStruct((1, channels), jnp.float32),
        in_specs=[pl.BlockSpec(memory_space=pltpu.VMEM)] * 2,
        out_specs=pl.BlockSpec(memory_space=pltpu.VMEM),
        scratch_shapes=[
            pltpu.VMEM((1, LANES), jnp.float32),
            pltpu.VMEM((devices, 1, LANES), jnp.float32),
            pltpu.SemaphoreType.DMA((devices,)),
            pltpu.SemaphoreType.DMA((devices,)),
        ],
        compiler_params=pltpu.CompilerParams(collective_id=0, has_side_effects=True),
        name="power",
    )(samples, channel_band.reshape(1, channels))

    blocks = channels // CB
    lag = top - delays
    first = (lag[:, ::CB] // VB).T
    last = (lag[:, CB - 1 :: CB] // VB).T
    count = last - first + 1
    inner_ends = jnp.cumsum(count, axis=1)
    totals = inner_ends[:, -1]
    evens = totals + totals % 2
    block_ends = jnp.cumsum(evens)
    starts = ((block_ends - evens)[:, None] + inner_ends - count).reshape(-1)
    first, last = first.reshape(-1), last.reshape(-1)
    spare = top // VB + 1
    step = 2 * UNROLL
    most = -(-(trials * (blocks + spare) + blocks) // step) * step
    item = jnp.arange(most, dtype=jnp.int32)
    index = jnp.arange(trials * blocks, dtype=jnp.int32)
    pair = jnp.sum((item[:, None] >= starts[None, :]).astype(jnp.int32), axis=1) - 1
    hit = pair[:, None] == index[None, :]
    tile = jnp.sum(jnp.where(hit, (first - starts)[None, :], 0), axis=1) + item
    inside = tile <= jnp.sum(jnp.where(hit, last[None, :], 0), axis=1)
    tile = jnp.where(inside, tile, spare)
    code = (pair % trials) + 32 * (pair // trials) + 1024 * tile
    n_iter = (block_ends[-1:] + (step - 1)) // step

    width = (spare + 1) * VB + SUB * rows
    smem = pl.BlockSpec(memory_space=pltpu.SMEM)
    vmem = pl.BlockSpec(memory_space=pltpu.VMEM)
    series = pl.pallas_call(
        spread_kernel,
        out_shape=jax.ShapeDtypeStruct((trials, width), jnp.float32),
        in_specs=[smem, smem, vmem, vmem, vmem],
        out_specs=vmem,
        scratch_shapes=[
            pltpu.VMEM((trials, 8, width), jnp.float32),
            pltpu.VMEM((rows, channels), jnp.bfloat16),
        ],
        name="spread",
    )(n_iter, code, samples, lag, gains)

    outer = width // LANES
    inner = bins * SUB // LANES
    reps = bins // inner
    k1 = jnp.arange(inner, dtype=jnp.int32)
    a = jnp.arange(outer, dtype=jnp.int32)
    b = jnp.arange(LANES, dtype=jnp.int32)
    k2 = jnp.arange(reps, dtype=jnp.int32)
    ang1 = (k1[:, None] * a[None, :] % inner).astype(jnp.float32) * (full_turn / inner)
    t3 = series.reshape(trials, outer, LANES)
    tab1 = jnp.stack([jnp.cos(ang1), -jnp.sin(ang1)])
    g = jnp.einsum("ika,dab->ikdb", tab1, t3, precision=lax.Precision.HIGH)
    ang2 = (k1[:, None] * b[None, :]).astype(jnp.float32) * (full_turn / period)
    c2, s2 = jnp.cos(ang2)[:, None, :], jnp.sin(ang2)[:, None, :]
    gr = g[0] * c2 + g[1] * s2
    gi = g[1] * c2 - g[0] * s2
    ang3 = (k2[:, None] * b[None, :] % LANES).astype(jnp.float32) * (full_turn / LANES)
    c3, s3 = jnp.cos(ang3), jnp.sin(ang3)
    gcat = jnp.concatenate([gr, gi], axis=2)
    tab3 = jnp.stack([jnp.concatenate([c3, s3], axis=1), jnp.concatenate([-s3, c3], axis=1)])
    d2 = jnp.einsum("kdb,irb->idrk", gcat, tab3, precision=lax.Precision.HIGH)
    d2 = d2.reshape(2, trials, bins)
    kk = jnp.arange(bins, dtype=jnp.int32)
    ang4 = (kk * (own * (SUB * rows) - top) % period).astype(jnp.float32) * (full_turn / period)
    c4, s4 = jnp.cos(ang4), jnp.sin(ang4)
    part = jnp.stack([d2[0] * c4 + d2[1] * s4, d2[1] * c4 - d2[0] * s4]).astype(jnp.bfloat16)

    taps = template_bank.shape[2]
    half = taps // 2
    split = part.reshape(2 * trials, devices, rows).transpose(1, 0, 2)
    ded = pl.pallas_call(
        functools.partial(gather_kernel, devices, half),
        out_shape=jax.ShapeDtypeStruct((2 * trials, rows + taps), jnp.float32),
        in_specs=[vmem],
        out_specs=vmem,
        scratch_shapes=[
            pltpu.VMEM((devices, 2 * trials, rows), jnp.bfloat16),
            pltpu.VMEM((2 * trials, rows), jnp.bfloat16),
            pltpu.VMEM((2 * trials, half), jnp.bfloat16),
            pltpu.VMEM((2 * trials, half), jnp.bfloat16),
            pltpu.SemaphoreType.DMA((devices,)),
            pltpu.SemaphoreType.DMA((devices,)),
            pltpu.SemaphoreType.DMA((4,)),
        ],
        compiler_params=pltpu.CompilerParams(collective_id=1, has_side_effects=True),
        name="gather",
    )(split)

    nz = template_ids.shape[0]
    selector = (template_ids[:, None] == jnp.arange(template_bank.shape[1], dtype=jnp.int32)[None, :]).astype(jnp.bfloat16)
    chosen = jnp.einsum("zb,ibt->izt", selector, template_bank[:, :, ::-1], preferred_element_type=jnp.float32)
    chosen = chosen.astype(jnp.bfloat16).reshape(2 * nz, taps)
    return pl.pallas_call(
        conv_kernel,
        out_shape=jax.ShapeDtypeStruct((trials, nz, rows), jnp.float32),
        in_specs=[vmem, vmem, vmem],
        out_specs=vmem,
        name="conv",
    )(chosen, ded[:trials], ded[trials:])


def solution(mesh):
    return jax.shard_map(
        per_device,
        mesh=mesh,
        in_specs=(P("tm", "beams"), P(), P(), P(), P()),
        out_specs=P("beams", None, "tm"),
        check_vma=False,
    )
```

```python
import functools
import math

import jax
import jax.numpy as jnp
import numpy as np
from jax import lax
from jax.experimental import pallas as pl
from jax.experimental.pallas import tpu as pltpu
from jax.sharding import PartitionSpec as P

NB = 16
SUB = 16
CB = 256
VB = 128
UNROLL = 32
CONV_UNROLL = 16
DFT_UNROLL = 4
LANES = 128
MESH = pl.DeviceIdType.MESH
full_turn = 2.0 * math.pi


def spread_kernel(n_ref, code_ref, s_ref, lag_ref, g_ref, out_ref, acc_ref, scaled_ref):
    rows, channels = s_ref.shape
    groups = rows // 8
    acc_ref[...] = jnp.zeros_like(acc_ref)
    lane = lax.broadcasted_iota(jnp.int32, (VB, CB), 0).astype(jnp.float32).astype(jnp.bfloat16)
    one = jnp.ones((VB, CB), jnp.bfloat16)
    zero = jnp.zeros((VB, CB), jnp.bfloat16)

    def scale(cb, carry):
        cols = pl.ds(pl.multiple_of(cb * CB, CB), CB)
        scaled_ref[:, cols] = (s_ref[:, cols].astype(jnp.float32) * g_ref[:, cols]).astype(jnp.bfloat16)
        return carry

    lax.fori_loop(0, channels // CB, scale, 0)

    def body(it, carry):
        for j in range(UNROLL):
            places, hots = [], []
            for half in range(2):
                code = code_ref[(it * UNROLL + j) * 2 + half]
                d = code & 31
                cb = (code >> 5) & 31
                vt = code >> 10
                cols = pl.ds(pl.multiple_of(cb * CB, CB), CB)
                lag = (lag_ref[pl.ds(d, 1), cols] - vt * VB).astype(jnp.float32)
                lag = jnp.broadcast_to(jnp.broadcast_to(lag, (16, CB)).astype(jnp.bfloat16)[None], (VB // 16, 16, CB)).reshape(VB, CB)
                hots.append(jnp.where(lag == lane, one, zero))
                places.append((d, vt))
            res = lax.dot_general(
                scaled_ref[:, cols],
                jnp.concatenate(hots, axis=0),
                (((1,), (1,)), ((), ())),
                preferred_element_type=jnp.float32,
            )
            for half, (d, vt) in enumerate(places):
                wide = jnp.concatenate(
                    [res[8 * g : 8 * g + 8, half * VB : (half + 1) * VB] for g in range(groups)], axis=1
                )
                at = pl.ds(pl.multiple_of(vt * VB, VB), groups * VB)
                acc_ref[d, :, at] += wide
        return carry

    lax.fori_loop(0, n_ref[0], body, 0)

    def finish(d, carry):
        x = acc_ref[d]
        x = pltpu.roll(x, 0, 1, stride=SUB, stride_axis=0)
        for n in range(out_ref.shape[1]):
            tile = x[:, n * LANES : (n + 1) * LANES]
            out_ref[d, n : n + 1, :] = jnp.sum(tile, axis=0, keepdims=True)
        return carry

    lax.fori_loop(0, out_ref.shape[0], finish, 0)


def greet(devices, me):
    barrier = pltpu.get_barrier_semaphore()

    def hello(i, carry):
        pl.semaphore_signal(barrier, inc=1, device_id={"tm": (me + i) % devices}, device_id_type=MESH)
        return carry

    lax.fori_loop(1, devices, hello, 0)
    return lambda: pl.semaphore_wait(barrier, devices - 1)


def power_kernel(devices, bins, s_ref, band_ref, gain_ref, mine_ref, got_ref, send_sem, recv_sem):
    me = lax.axis_index("tm")
    rows, channels = s_ref.shape
    arrived = greet(devices, me)
    band = band_ref[...]
    hit = band == lax.broadcasted_iota(jnp.int32, (NB, channels), 0)
    part = 256
    squares = []
    for c in range(0, channels, part):
        x = s_ref[:, c : c + part].astype(jnp.float32)
        squares.append(jnp.sum(x * x, axis=0, keepdims=True))
    squares = jnp.concatenate(squares, axis=1)
    power = jnp.sum(jnp.where(hit, squares, 0.0), axis=1, keepdims=True)
    members = jnp.sum(jnp.where(hit, 1.0, 0.0), axis=1, keepdims=True)
    eye = lax.broadcasted_iota(jnp.int32, (NB, LANES), 0) == lax.broadcasted_iota(jnp.int32, (NB, LANES), 1)
    mine_ref[...] = jnp.sum(jnp.where(eye, power, 0.0), axis=0, keepdims=True)
    arrived()

    def copy_to(peer, slot):
        return pltpu.make_async_remote_copy(
            src_ref=mine_ref,
            dst_ref=got_ref.at[slot],
            send_sem=send_sem.at[peer],
            recv_sem=recv_sem.at[slot],
            device_id={"tm": peer},
            device_id_type=MESH,
        )

    def send(i, carry):
        copy_to((me + i) % devices, me).start()
        return carry

    lax.fori_loop(1, devices, send, 0)

    def take(i, total):
        q = (me + devices - i) % devices
        copy_to(q, q).wait_recv()
        return total + got_ref[q]

    total = lax.fori_loop(1, devices, take, mine_ref[...])
    column = jnp.sum(jnp.where(eye, total, 0.0), axis=1, keepdims=True)
    band_gain = 1.0 / (jnp.sqrt(column / (members * bins) + 1e-06) * math.sqrt(channels * bins))
    gain_ref[...] = jnp.sum(jnp.where(hit, band_gain, 0.0), axis=0, keepdims=True)

    def sent(i, carry):
        copy_to((me + i) % devices, me).wait_send()
        return carry

    lax.fori_loop(1, devices, sent, 0)


def exact_dot(left, right, dims):
    left_hi = left.astype(jnp.bfloat16)
    right_hi = right.astype(jnp.bfloat16)
    left_lo = (left - left_hi.astype(jnp.float32)).astype(jnp.bfloat16)
    right_lo = (right - right_hi.astype(jnp.float32)).astype(jnp.bfloat16)
    dot = functools.partial(
        lax.dot_general, dimension_numbers=(dims, ((), ())), preferred_element_type=jnp.float32
    )
    return dot(left_hi, right_hi) + (dot(left_hi, right_lo) + dot(left_lo, right_hi))


def gather_kernel(
    devices, half, series_ref, tab1_ref, tab2_ref, tab3_ref, tab4_ref,
    out_ref, stage_ref, part_ref, got_ref, mine_ref, left_ref, right_ref, send_sem, recv_sem, halo_sem,
):
    me = lax.axis_index("tm")
    rows = part_ref.shape[2]
    trials, outer, lanes = series_ref.shape
    inner = tab2_ref.shape[1]
    reps = tab4_ref.shape[1]
    per = inner // rows
    arrived = greet(devices, me)

    def transform(d):
        g = exact_dot(tab1_ref[...], series_ref[d], ((1,), (0,)))
        g_re, g_im = g[:inner], g[inner:]
        c2, s2 = tab2_ref[0], tab2_ref[1]
        both = jnp.concatenate([g_re * c2 + g_im * s2, g_im * c2 - g_re * s2], axis=1)
        e = exact_dot(tab3_ref[...], both, ((1,), (1,)))
        e_re, e_im = e[:reps], e[reps:]
        c4, s4 = tab4_ref[0], tab4_ref[1]
        for n, value in enumerate((e_re * c4 + e_im * s4, e_im * c4 - e_re * s4)):
            for r in range(reps):
                for p in range(per):
                    row = value[r : r + 1, p * rows : (p + 1) * rows]
                    stage_ref[r * per + p, pl.ds(n * trials + d, 1), :] = row

    def some(i, carry):
        for j in range(DFT_UNROLL):
            transform(i * DFT_UNROLL + j)
        return carry

    lax.fori_loop(0, trials // DFT_UNROLL, some, 0)

    def narrow(i, carry):
        part_ref[i] = stage_ref[i].astype(jnp.bfloat16)
        return carry

    lax.fori_loop(0, devices, narrow, 0)
    arrived()

    def copy_to(peer, slot):
        return pltpu.make_async_remote_copy(
            src_ref=part_ref.at[peer],
            dst_ref=got_ref.at[slot],
            send_sem=send_sem.at[peer],
            recv_sem=recv_sem.at[slot],
            device_id={"tm": peer},
            device_id_type=MESH,
        )

    def send(i, carry):
        copy_to((me + i) % devices, me).start()
        return carry

    lax.fori_loop(1, devices, send, 0)

    def take(i, total):
        q = (me + devices - i) % devices
        copy_to(q, q).wait_recv()
        return total + got_ref[q].astype(jnp.float32)

    total = lax.fori_loop(1, devices, take, part_ref[me].astype(jnp.float32)).astype(jnp.bfloat16)
    mine_ref[...] = total
    halos = []
    for n, (peer, source, target) in enumerate(
        (
            ((me + 1) % devices, mine_ref.at[:, rows - half :], left_ref),
            ((me + devices - 1) % devices, mine_ref.at[:, :half], right_ref),
        )
    ):
        copy = pltpu.make_async_remote_copy(
            src_ref=source,
            dst_ref=target,
            send_sem=halo_sem.at[2 * n],
            recv_sem=halo_sem.at[2 * n + 1],
            device_id={"tm": peer},
            device_id_type=MESH,
        )
        copy.start()
        halos.append(copy)
    out_ref[:, half : half + rows] = total.astype(jnp.float32)

    def sent(i, carry):
        copy_to((me + i) % devices, me).wait_send()
        return carry

    lax.fori_loop(1, devices, sent, 0)
    for copy in halos:
        copy.wait()
    out_ref[:, :half] = left_ref[...].astype(jnp.float32)
    out_ref[:, half + rows :] = right_ref[...].astype(jnp.float32)


def conv_kernel(h_ref, x_ref, out_ref):
    taps = h_ref.shape[1]
    nz = h_ref.shape[0] // 2
    trials, span = x_ref.shape[0] // 2, x_ref.shape[1]
    width = span - taps

    def one(d):
        cols = []
        for row in (d, trials + d):
            x = jnp.broadcast_to(x_ref[pl.ds(row, 1), :], (taps, span))
            x = pltpu.roll(x, span - taps + 1, 1, stride=1, stride_axis=0)
            cols.append(x[:, :width].astype(jnp.bfloat16))
        res = jnp.dot(h_ref[...], jnp.concatenate(cols, axis=1), preferred_element_type=jnp.float32)
        a_re = res[:nz, :width] - res[nz:, width:]
        a_im = res[:nz, width:] + res[nz:, :width]
        out_ref[d] = a_re * a_re + a_im * a_im

    def body(i, carry):
        for j in range(CONV_UNROLL):
            one(i * CONV_UNROLL + j)
        return carry

    lax.fori_loop(0, trials // CONV_UNROLL, body, 0)


def per_device(samples, channel_band, delays, template_bank, template_ids):
    rows, channels = samples.shape
    trials = delays.shape[0]
    devices = lax.axis_size("tm")
    bins = rows * devices
    period = SUB * bins
    top = bins * 4
    own = lax.axis_index("tm")

    gains = pl.pallas_call(
        functools.partial(power_kernel, devices, bins),
        out_shape=jax.ShapeDtypeStruct((1, channels), jnp.float32),
        in_specs=[pl.BlockSpec(memory_space=pltpu.VMEM)] * 2,
        out_specs=pl.BlockSpec(memory_space=pltpu.VMEM),
        scratch_shapes=[
            pltpu.VMEM((1, LANES), jnp.float32),
            pltpu.VMEM((devices, 1, LANES), jnp.float32),
            pltpu.SemaphoreType.DMA((devices,)),
            pltpu.SemaphoreType.DMA((devices,)),
        ],
        compiler_params=pltpu.CompilerParams(collective_id=0, has_side_effects=True),
        name="power",
    )(samples, channel_band.reshape(1, channels))

    blocks = channels // CB
    lag = top - delays
    first = (lag[:, ::CB] // VB).T
    last = (lag[:, CB - 1 :: CB] // VB).T
    count = last - first + 1
    inner_ends = jnp.cumsum(count, axis=1)
    totals = inner_ends[:, -1]
    evens = totals + totals % 2
    block_ends = jnp.cumsum(evens)
    starts = ((block_ends - evens)[:, None] + inner_ends - count).reshape(-1)
    first, last = first.reshape(-1), last.reshape(-1)
    spare = top // VB + 1
    step = 2 * UNROLL
    most = -(-(trials * (blocks + spare) + blocks) // step) * step
    item = jnp.arange(most, dtype=jnp.int32)
    index = jnp.arange(trials * blocks, dtype=jnp.int32)
    pair = jnp.sum((item[:, None] >= starts[None, :]).astype(jnp.int32), axis=1) - 1
    hit = pair[:, None] == index[None, :]
    tile = jnp.sum(jnp.where(hit, (first - starts)[None, :], 0), axis=1) + item
    inside = tile <= jnp.sum(jnp.where(hit, last[None, :], 0), axis=1)
    tile = jnp.where(inside, tile, spare)
    code = (pair % trials) + 32 * (pair // trials) + 1024 * tile
    n_iter = (block_ends[-1:] + (step - 1)) // step

    width = (spare + 1) * VB + SUB * rows
    smem = pl.BlockSpec(memory_space=pltpu.SMEM)
    vmem = pl.BlockSpec(memory_space=pltpu.VMEM)
    series = pl.pallas_call(
        spread_kernel,
        out_shape=jax.ShapeDtypeStruct((trials, width // LANES, LANES), jnp.float32),
        in_specs=[smem, smem, vmem, vmem, vmem],
        out_specs=vmem,
        scratch_shapes=[
            pltpu.VMEM((trials, 8, width), jnp.float32),
            pltpu.VMEM((rows, channels), jnp.bfloat16),
        ],
        name="spread",
    )(n_iter, code, samples, lag, gains)

    outer = width // LANES
    inner = bins * SUB // LANES
    reps = bins // inner
    k1 = np.arange(inner)
    a = np.arange(outer)
    b = np.arange(LANES)
    k2 = np.arange(reps)
    ang1 = (k1[:, None] * a[None, :] % inner) * (full_turn / inner)
    tab1 = np.concatenate([np.cos(ang1), -np.sin(ang1)]).astype(np.float32)
    ang2 = (k1[:, None] * b[None, :]) * (full_turn / period)
    tab2 = np.stack([np.cos(ang2), np.sin(ang2)]).astype(np.float32)
    ang3 = (k2[:, None] * b[None, :] % LANES) * (full_turn / LANES)
    c3, s3 = np.cos(ang3), np.sin(ang3)
    tab3 = np.concatenate(
        [np.concatenate([c3, s3], axis=1), np.concatenate([-s3, c3], axis=1)]
    ).astype(np.float32)
    kk = jnp.arange(bins, dtype=jnp.int32)
    ang4 = (kk * (own * (SUB * rows) - top) % period).astype(jnp.float32) * (full_turn / period)
    tab4 = jnp.stack([jnp.cos(ang4), jnp.sin(ang4)]).reshape(2, reps, inner)

    taps = template_bank.shape[2]
    half = taps // 2
    ded = pl.pallas_call(
        functools.partial(gather_kernel, devices, half),
        out_shape=jax.ShapeDtypeStruct((2 * trials, rows + taps), jnp.float32),
        in_specs=[vmem] * 5,
        out_specs=vmem,
        scratch_shapes=[
            pltpu.VMEM((devices, 2 * trials, rows), jnp.float32),
            pltpu.VMEM((devices, 2 * trials, rows), jnp.bfloat16),
            pltpu.VMEM((devices, 2 * trials, rows), jnp.bfloat16),
            pltpu.VMEM((2 * trials, rows), jnp.bfloat16),
            pltpu.VMEM((2 * trials, half), jnp.bfloat16),
            pltpu.VMEM((2 * trials, half), jnp.bfloat16),
            pltpu.SemaphoreType.DMA((devices,)),
            pltpu.SemaphoreType.DMA((devices,)),
            pltpu.SemaphoreType.DMA((4,)),
        ],
        compiler_params=pltpu.CompilerParams(collective_id=1, has_side_effects=True),
        name="gather",
    )(series, jnp.asarray(tab1), jnp.asarray(tab2), jnp.asarray(tab3), tab4)

    nz = template_ids.shape[0]
    selector = (template_ids[:, None] == jnp.arange(template_bank.shape[1], dtype=jnp.int32)[None, :]).astype(jnp.bfloat16)
    chosen = jnp.einsum("zb,ibt->izt", selector, template_bank[:, :, ::-1], preferred_element_type=jnp.float32)
    chosen = chosen.astype(jnp.bfloat16).reshape(2 * nz, taps)
    return pl.pallas_call(
        conv_kernel,
        out_shape=jax.ShapeDtypeStruct((trials, nz, rows), jnp.float32),
        in_specs=[vmem, vmem],
        out_specs=vmem,
        name="conv",
    )(chosen, ded)


def solution(mesh):
    return jax.shard_map(
        per_device,
        mesh=mesh,
        in_specs=(P("tm", "beams"), P(), P(), P(), P()),
        out_specs=P("beams", None, "tm"),
        check_vma=False,
    )
```

```python
import functools
import math

import jax
import jax.numpy as jnp
import numpy as np
from jax import lax
from jax.experimental import pallas as pl
from jax.experimental.pallas import tpu as pltpu
from jax.sharding import PartitionSpec as P

NB = 16
SUB = 16
CB = 256
VB = 128
UNROLL = 32
CONV_UNROLL = 16
DFT_UNROLL = 4
LANES = 128
MESH = pl.DeviceIdType.MESH
full_turn = 2.0 * math.pi


def spread_kernel(n_ref, code_ref, s_ref, lag_ref, g_ref, out_ref, acc_ref, scaled_ref):
    rows, channels = s_ref.shape
    groups = rows // 8
    acc_ref[...] = jnp.zeros_like(acc_ref)
    lane = lax.broadcasted_iota(jnp.int32, (VB, CB), 0).astype(jnp.float32).astype(jnp.bfloat16)
    one = jnp.ones((VB, CB), jnp.bfloat16)
    zero = jnp.zeros((VB, CB), jnp.bfloat16)

    def scale(cb, carry):
        cols = pl.ds(pl.multiple_of(cb * CB, CB), CB)
        scaled_ref[:, cols] = (s_ref[:, cols].astype(jnp.float32) * g_ref[:, cols]).astype(jnp.bfloat16)
        return carry

    lax.fori_loop(0, channels // CB, scale, 0)

    def body(it, carry):
        for j in range(UNROLL):
            places, hots = [], []
            for half in range(2):
                code = code_ref[(it * UNROLL + j) * 2 + half]
                d = code & 31
                cb = (code >> 5) & 31
                vt = code >> 10
                cols = pl.ds(pl.multiple_of(cb * CB, CB), CB)
                lag = (lag_ref[pl.ds(d, 1), cols] - vt * VB).astype(jnp.float32)
                lag = jnp.broadcast_to(jnp.broadcast_to(lag, (16, CB)).astype(jnp.bfloat16)[None], (VB // 16, 16, CB)).reshape(VB, CB)
                hots.append(jnp.where(lag == lane, one, zero))
                places.append((d, vt))
            res = lax.dot_general(
                scaled_ref[:, cols],
                jnp.concatenate(hots, axis=0),
                (((1,), (1,)), ((), ())),
                preferred_element_type=jnp.float32,
            )
            for half, (d, vt) in enumerate(places):
                wide = jnp.concatenate(
                    [res[8 * g : 8 * g + 8, half * VB : (half + 1) * VB] for g in range(groups)], axis=1
                )
                at = pl.ds(pl.multiple_of(vt * VB, VB), groups * VB)
                acc_ref[d, :, at] += wide
        return carry

    lax.fori_loop(0, n_ref[0], body, 0)

    def finish(d, carry):
        x = acc_ref[d]
        x = pltpu.roll(x, 0, 1, stride=SUB, stride_axis=0)
        for n in range(out_ref.shape[1]):
            tile = x[:, n * LANES : (n + 1) * LANES]
            out_ref[d, n : n + 1, :] = jnp.sum(tile, axis=0, keepdims=True)
        return carry

    lax.fori_loop(0, out_ref.shape[0], finish, 0)


def greet(devices, me):
    barrier = pltpu.get_barrier_semaphore()

    def hello(i, carry):
        pl.semaphore_signal(barrier, inc=1, device_id={"tm": (me + i) % devices}, device_id_type=MESH)
        return carry

    lax.fori_loop(1, devices, hello, 0)
    return lambda: pl.semaphore_wait(barrier, devices - 1)


def power_kernel(devices, bins, s_ref, band_ref, gain_ref, mine_ref, got_ref, send_sem, recv_sem):
    me = lax.axis_index("tm")
    rows, channels = s_ref.shape
    arrived = greet(devices, me)
    band = band_ref[...]
    hit = band == lax.broadcasted_iota(jnp.int32, (NB, channels), 0)
    part = 256
    squares = []
    for c in range(0, channels, part):
        x = s_ref[:, c : c + part].astype(jnp.float32)
        squares.append(jnp.sum(x * x, axis=0, keepdims=True))
    squares = jnp.concatenate(squares, axis=1)
    power = jnp.sum(jnp.where(hit, squares, 0.0), axis=1, keepdims=True)
    members = jnp.sum(jnp.where(hit, 1.0, 0.0), axis=1, keepdims=True)
    eye = lax.broadcasted_iota(jnp.int32, (NB, LANES), 0) == lax.broadcasted_iota(jnp.int32, (NB, LANES), 1)
    mine_ref[...] = jnp.sum(jnp.where(eye, power, 0.0), axis=0, keepdims=True)
    arrived()

    def copy_to(peer, slot):
        return pltpu.make_async_remote_copy(
            src_ref=mine_ref,
            dst_ref=got_ref.at[slot],
            send_sem=send_sem.at[peer],
            recv_sem=recv_sem.at[slot],
            device_id={"tm": peer},
            device_id_type=MESH,
        )

    def send(i, carry):
        copy_to((me + i) % devices, me).start()
        return carry

    lax.fori_loop(1, devices, send, 0)

    def take(i, total):
        q = (me + devices - i) % devices
        copy_to(q, q).wait_recv()
        return total + got_ref[q]

    total = lax.fori_loop(1, devices, take, mine_ref[...])
    column = jnp.sum(jnp.where(eye, total, 0.0), axis=1, keepdims=True)
    band_gain = 1.0 / (jnp.sqrt(column / (members * bins) + 1e-06) * math.sqrt(channels * bins))
    gain_ref[...] = jnp.sum(jnp.where(hit, band_gain, 0.0), axis=0, keepdims=True)

    def sent(i, carry):
        copy_to((me + i) % devices, me).wait_send()
        return carry

    lax.fori_loop(1, devices, sent, 0)


def exact_dot(left, right, dims):
    left_hi = left.astype(jnp.bfloat16)
    right_hi = right.astype(jnp.bfloat16)
    left_lo = (left - left_hi.astype(jnp.float32)).astype(jnp.bfloat16)
    right_lo = (right - right_hi.astype(jnp.float32)).astype(jnp.bfloat16)
    dot = functools.partial(
        lax.dot_general, dimension_numbers=(dims, ((), ())), preferred_element_type=jnp.float32
    )
    return dot(left_hi, right_hi) + (dot(left_hi, right_lo) + dot(left_lo, right_hi))


def gather_kernel(
    devices, half, series_ref, tab1_ref, tab2_ref, tab3_ref, tab4_ref,
    out_ref, stage_ref, part_ref, got_ref, mine_ref, left_ref, right_ref, send_sem, recv_sem, halo_sem,
):
    me = lax.axis_index("tm")
    rows = part_ref.shape[2]
    trials, outer, lanes = series_ref.shape
    inner = tab2_ref.shape[1]
    reps = tab4_ref.shape[1]
    per = inner // rows
    arrived = greet(devices, me)

    def transform(d):
        g = exact_dot(tab1_ref[...], series_ref[d], ((1,), (0,)))
        g_re, g_im = g[:inner], g[inner:]
        c2, s2 = tab2_ref[0], tab2_ref[1]
        both = jnp.concatenate([g_re * c2 + g_im * s2, g_im * c2 - g_re * s2], axis=1)
        e = exact_dot(tab3_ref[...], both, ((1,), (1,)))
        e_re, e_im = e[:reps], e[reps:]
        c4, s4 = tab4_ref[0], tab4_ref[1]
        for n, value in enumerate((e_re * c4 + e_im * s4, e_im * c4 - e_re * s4)):
            for r in range(reps):
                for p in range(per):
                    row = value[r : r + 1, p * rows : (p + 1) * rows]
                    stage_ref[r * per + p, pl.ds(n * trials + d, 1), :] = row

    def some(i, carry):
        for j in range(DFT_UNROLL):
            transform(i * DFT_UNROLL + j)
        return carry

    lax.fori_loop(0, trials // DFT_UNROLL, some, 0)

    def narrow(i, carry):
        part_ref[i] = stage_ref[i].astype(jnp.bfloat16)
        return carry

    lax.fori_loop(0, devices, narrow, 0)
    arrived()

    def copy_to(peer, slot):
        return pltpu.make_async_remote_copy(
            src_ref=part_ref.at[peer],
            dst_ref=got_ref.at[slot],
            send_sem=send_sem.at[peer],
            recv_sem=recv_sem.at[slot],
            device_id={"tm": peer},
            device_id_type=MESH,
        )

    def send(i, carry):
        copy_to((me + i) % devices, me).start()
        return carry

    lax.fori_loop(1, devices, send, 0)

    def take(i, total):
        q = (me + devices - i) % devices
        copy_to(q, q).wait_recv()
        return total + got_ref[q].astype(jnp.float32)

    total = lax.fori_loop(1, devices, take, part_ref[me].astype(jnp.float32)).astype(jnp.bfloat16)
    mine_ref[...] = total
    halos = []
    for n, (peer, source, target) in enumerate(
        (
            ((me + 1) % devices, mine_ref.at[:, rows - half :], left_ref),
            ((me + devices - 1) % devices, mine_ref.at[:, :half], right_ref),
        )
    ):
        copy = pltpu.make_async_remote_copy(
            src_ref=source,
            dst_ref=target,
            send_sem=halo_sem.at[2 * n],
            recv_sem=halo_sem.at[2 * n + 1],
            device_id={"tm": peer},
            device_id_type=MESH,
        )
        copy.start()
        halos.append(copy)
    out_ref[:, half : half + rows] = total.astype(jnp.float32)

    def sent(i, carry):
        copy_to((me + i) % devices, me).wait_send()
        return carry

    lax.fori_loop(1, devices, sent, 0)
    for copy in halos:
        copy.wait()
    out_ref[:, :half] = left_ref[...].astype(jnp.float32)
    out_ref[:, half + rows :] = right_ref[...].astype(jnp.float32)


def conv_kernel(ids_ref, bank_ref, x_ref, out_ref, h_ref):
    taps = h_ref.shape[1]
    nz = h_ref.shape[0] // 2
    trials, span = x_ref.shape[0] // 2, x_ref.shape[1]
    width = span - taps
    entries = bank_ref.shape[1]
    pick = lax.broadcasted_iota(jnp.int32, (entries, nz), 0) == ids_ref[...]
    pick = jnp.where(pick, 1.0, 0.0).astype(jnp.bfloat16)
    flip = lax.broadcasted_iota(jnp.int32, (taps, taps), 0) + lax.broadcasted_iota(jnp.int32, (taps, taps), 1)
    flip = jnp.where(flip == taps - 1, 1.0, 0.0).astype(jnp.bfloat16)
    for n in range(2):
        chosen = lax.dot_general(
            pick, bank_ref[n], (((0,), (0,)), ((), ())), preferred_element_type=jnp.float32
        ).astype(jnp.bfloat16)
        h_ref[n * nz : (n + 1) * nz, :] = jnp.dot(
            chosen, flip, preferred_element_type=jnp.float32
        ).astype(jnp.bfloat16)

    def one(d):
        cols = []
        for row in (d, trials + d):
            x = jnp.broadcast_to(x_ref[pl.ds(row, 1), :], (taps, span))
            x = pltpu.roll(x, span - taps + 1, 1, stride=1, stride_axis=0)
            cols.append(x[:, :width].astype(jnp.bfloat16))
        res = jnp.dot(h_ref[...], jnp.concatenate(cols, axis=1), preferred_element_type=jnp.float32)
        a_re = res[:nz, :width] - res[nz:, width:]
        a_im = res[:nz, width:] + res[nz:, :width]
        out_ref[d] = a_re * a_re + a_im * a_im

    def body(i, carry):
        for j in range(CONV_UNROLL):
            one(i * CONV_UNROLL + j)
        return carry

    lax.fori_loop(0, trials // CONV_UNROLL, body, 0)


def per_device(samples, channel_band, delays, template_bank, template_ids):
    rows, channels = samples.shape
    trials = delays.shape[0]
    devices = lax.axis_size("tm")
    bins = rows * devices
    period = SUB * bins
    top = bins * 4
    own = lax.axis_index("tm")

    gains = pl.pallas_call(
        functools.partial(power_kernel, devices, bins),
        out_shape=jax.ShapeDtypeStruct((1, channels), jnp.float32),
        in_specs=[pl.BlockSpec(memory_space=pltpu.VMEM)] * 2,
        out_specs=pl.BlockSpec(memory_space=pltpu.VMEM),
        scratch_shapes=[
            pltpu.VMEM((1, LANES), jnp.float32),
            pltpu.VMEM((devices, 1, LANES), jnp.float32),
            pltpu.SemaphoreType.DMA((devices,)),
            pltpu.SemaphoreType.DMA((devices,)),
        ],
        compiler_params=pltpu.CompilerParams(collective_id=0, has_side_effects=True),
        name="power",
    )(samples, channel_band.reshape(1, channels))

    blocks = channels // CB
    lag = top - delays
    first = (lag[:, ::CB] // VB).T
    last = (lag[:, CB - 1 :: CB] // VB).T
    count = last - first + 1
    inner_ends = jnp.cumsum(count, axis=1)
    totals = inner_ends[:, -1]
    evens = totals + totals % 2
    block_ends = jnp.cumsum(evens)
    starts = ((block_ends - evens)[:, None] + inner_ends - count).reshape(-1)
    first, last = first.reshape(-1), last.reshape(-1)
    spare = top // VB + 1
    step = 2 * UNROLL
    most = -(-(trials * (blocks + spare) + blocks) // step) * step
    item = jnp.arange(most, dtype=jnp.int32)
    index = jnp.arange(trials * blocks, dtype=jnp.int32)
    pair = jnp.sum((item[:, None] >= starts[None, :]).astype(jnp.int32), axis=1) - 1
    hit = pair[:, None] == index[None, :]
    tile = jnp.sum(jnp.where(hit, (first - starts)[None, :], 0), axis=1) + item
    inside = tile <= jnp.sum(jnp.where(hit, last[None, :], 0), axis=1)
    tile = jnp.where(inside, tile, spare)
    code = (pair % trials) + 32 * (pair // trials) + 1024 * tile
    n_iter = (block_ends[-1:] + (step - 1)) // step

    width = (spare + 1) * VB + SUB * rows
    smem = pl.BlockSpec(memory_space=pltpu.SMEM)
    vmem = pl.BlockSpec(memory_space=pltpu.VMEM)
    series = pl.pallas_call(
        spread_kernel,
        out_shape=jax.ShapeDtypeStruct((trials, width // LANES, LANES), jnp.float32),
        in_specs=[smem, smem, vmem, vmem, vmem],
        out_specs=vmem,
        scratch_shapes=[
            pltpu.VMEM((trials, 8, width), jnp.float32),
            pltpu.VMEM((rows, channels), jnp.bfloat16),
        ],
        name="spread",
    )(n_iter, code, samples, lag, gains)

    outer = width // LANES
    inner = bins * SUB // LANES
    reps = bins // inner
    k1 = np.arange(inner)
    a = np.arange(outer)
    b = np.arange(LANES)
    k2 = np.arange(reps)
    ang1 = (k1[:, None] * a[None, :] % inner) * (full_turn / inner)
    tab1 = np.concatenate([np.cos(ang1), -np.sin(ang1)]).astype(np.float32)
    ang2 = (k1[:, None] * b[None, :]) * (full_turn / period)
    tab2 = np.stack([np.cos(ang2), np.sin(ang2)]).astype(np.float32)
    ang3 = (k2[:, None] * b[None, :] % LANES) * (full_turn / LANES)
    c3, s3 = np.cos(ang3), np.sin(ang3)
    tab3 = np.concatenate(
        [np.concatenate([c3, s3], axis=1), np.concatenate([-s3, c3], axis=1)]
    ).astype(np.float32)
    kk = jnp.arange(bins, dtype=jnp.int32)
    ang4 = (kk * (own * (SUB * rows) - top) % period).astype(jnp.float32) * (full_turn / period)
    tab4 = jnp.stack([jnp.cos(ang4), jnp.sin(ang4)]).reshape(2, reps, inner)

    taps = template_bank.shape[2]
    half = taps // 2
    ded = pl.pallas_call(
        functools.partial(gather_kernel, devices, half),
        out_shape=jax.ShapeDtypeStruct((2 * trials, rows + taps), jnp.float32),
        in_specs=[vmem] * 5,
        out_specs=vmem,
        scratch_shapes=[
            pltpu.VMEM((devices, 2 * trials, rows), jnp.float32),
            pltpu.VMEM((devices, 2 * trials, rows), jnp.bfloat16),
            pltpu.VMEM((devices, 2 * trials, rows), jnp.bfloat16),
            pltpu.VMEM((2 * trials, rows), jnp.bfloat16),
            pltpu.VMEM((2 * trials, half), jnp.bfloat16),
            pltpu.VMEM((2 * trials, half), jnp.bfloat16),
            pltpu.SemaphoreType.DMA((devices,)),
            pltpu.SemaphoreType.DMA((devices,)),
            pltpu.SemaphoreType.DMA((4,)),
        ],
        compiler_params=pltpu.CompilerParams(collective_id=1, has_side_effects=True),
        name="gather",
    )(series, jnp.asarray(tab1), jnp.asarray(tab2), jnp.asarray(tab3), tab4)

    nz = template_ids.shape[0]
    return pl.pallas_call(
        conv_kernel,
        out_shape=jax.ShapeDtypeStruct((trials, nz, rows), jnp.float32),
        in_specs=[vmem] * 3,
        out_specs=vmem,
        scratch_shapes=[pltpu.VMEM((2 * nz, taps), jnp.bfloat16)],
        name="conv",
    )(template_ids.reshape(1, nz), template_bank, ded)


def solution(mesh):
    return jax.shard_map(
        per_device,
        mesh=mesh,
        in_specs=(P("tm", "beams"), P(), P(), P(), P()),
        out_specs=P("beams", None, "tm"),
        check_vma=False,
    )
```
